32 devices in a mesh: atoms: 16 (over z, x, core), grid: 2 (over y).
Axes of the slice: x: 2, y: 2, z: 4, core: 2. Of those that a mesh axis runs over, the one named last changes fastest.
Arguments:
- basis_values: bfloat16 [16, 2, 2048, 1152], P('atoms', 'grid'), may hold values from -6 to 6
- potential: float32 [16, 2, 2048], P('atoms', 'grid'), may hold values from -6 to 6
- block_lists: int32 [16, 2, 6], P('atoms', 'grid'), may hold values from -1 to 8, as said below
Outputs:
- density_columns: float32 [16, 2, 768, 128], P('atoms', 'grid')
The draws below stay inside these ranges and needn't reach their ends.
Inputs may be any that keep to these rules, and one draw needn't show every extreme that they name: `block_lists`: entry 0 of every cell's list is 4, the cell itself. For some m from 4 to 6, entries 1 to m - 1 are distinct codes other than 4 whose neighbour cell lies on the line (line positions 0 to 1), and entries from m on are -1. Some cell has m = 6.
All inputs are finite; a program needn't handle non-finite values.
Results may differ from the reference program's by a relative error of at most 0.0017.
Values sent between devices are 32-bit elements; how exact they have to be, the bound alone decides.
No kernel may reach another device: no remote copies, remote signals or barrier semaphores. Data moves between devices by JAX's collectives and lax.ppermute only.
A program may use at most 64 MiB of HBM per device.

```python
import jax
import jax.numpy as jnp
from jax import lax

B = 128
POINTS = 2048
MAXB = 6
ITERS = 3
REGIONS = 16
LINES = 2


def draw_block_lists(key, part):
    cell_total = REGIONS * LINES
    key_scores, key_counts = jax.random.split(jax.random.fold_in(key, 17))
    others = jnp.array([0, 1, 2, 3, 5, 6, 7, 8], dtype=jnp.int32)
    raw_scores = jax.random.randint(key_scores, (cell_total, 8), 0, 1 << 20, dtype=jnp.int32)
    scores = raw_scores * 16 + jnp.arange(8, dtype=jnp.int32)[None, :]
    line_pos = jnp.arange(cell_total, dtype=jnp.int32) % LINES
    reached = line_pos[:, None] + (others % 3 - 1)[None, :]
    outside = (reached < 0) | (reached >= LINES)
    scores = jnp.where(outside, scores - (1 << 26), scores)
    best_scores, best_index = lax.top_k(scores, 5)
    chosen = others[best_index]
    block_counts = jax.random.randint(key_counts, (cell_total,), MAXB - 2, MAXB + 1, dtype=jnp.int32)
    block_counts = block_counts.at[0].set(MAXB)
    slot_pos = jnp.arange(MAXB - 1, dtype=jnp.int32)
    tail_codes = jnp.where(slot_pos[None, :] < block_counts[:, None] - 1, chosen[:, :MAXB - 1], -1)
    code_lists = jnp.concatenate([jnp.full((cell_total, 1), 4, dtype=jnp.int32), tail_codes], axis=1)
    return code_lists.reshape(REGIONS, LINES, MAXB).astype(jnp.int32)


def steps_of(stream_key, dims, shards, smallest, top_value):
    level = 1.0
    for dim, parts in shards:
        heights = jax.random.uniform(jax.random.fold_in(jax.random.fold_in(stream_key, 6), dim), (parts,), jnp.float32, smallest / len(shards), top_value / len(shards))
        level = level * jnp.repeat(jnp.exp(heights), dims[dim] // parts).reshape((-1,) + (1,) * (len(dims) - 1 - dim))
    return level


def centred(rng, shape, width, reach, cuts=(), kind=jnp.bfloat16):
    loudness = steps_of(rng, shape, cuts, -0.22, 0.18) if cuts else 1.0
    entries = jax.random.normal(rng, shape, jnp.float32) * width * loudness
    return jnp.minimum(jnp.maximum(entries, -reach), reach).astype(kind)


def setup_inputs(seed: int = 0) -> dict:
    streams_of = jax.random.split(jax.random.key(seed), 4)
    basis_values = centred(streams_of[0], (REGIONS, LINES, POINTS, 9 * B), 1.0, 6.0, ((0, 16), (1, 2)))
    potential = centred(streams_of[1], (REGIONS, LINES, POINTS), 1.0, 6.0, ((0, 16), (1, 2)), jnp.float32)
    block_lists = draw_block_lists(jax.random.fold_in(streams_of[3], 71), 0)
    return {"basis_values": basis_values, "potential": potential, "block_lists": block_lists}


def newton_sign(submatrix, live_blocks, block_size):
    padded = submatrix.shape[0]
    position = jnp.arange(padded, dtype=jnp.int32)
    active = (position // block_size < live_blocks).astype(jnp.float32)
    live_count = (live_blocks * block_size).astype(jnp.float32)
    mean_level = jnp.trace(submatrix) / live_count
    shifted = (mean_level * jnp.diag(active) - submatrix) * active[:, None] * active[None, :]
    normal_form = shifted * (lax.rsqrt(jnp.sum(shifted * shifted) + 1e-06) * jnp.sqrt(live_count))
    square_form = jnp.dot(normal_form, normal_form, precision=lax.Precision.HIGHEST)
    fourth_form = jnp.dot(square_form, square_form, precision=lax.Precision.HIGHEST)
    bound_value = jnp.sqrt(jnp.sqrt(jnp.sqrt(jnp.sum(fourth_form * fourth_form) + 1e-06)))
    current = normal_form / bound_value
    square = square_form / (bound_value * bound_value)
    for sweep in range(ITERS - 1):
        if sweep > 0:
            square = jnp.dot(current, current, precision=lax.Precision.HIGHEST)
        current = 1.5 * current - 0.5 * jnp.dot(current, square, precision=lax.Precision.HIGHEST)
    columns = current[:, :block_size]
    inner_cols = jnp.dot(current, columns, precision=lax.Precision.HIGHEST)
    sign_cols = 1.5 * columns - 0.5 * jnp.dot(current, inner_cols, precision=lax.Precision.HIGHEST)
    unit_cols = (position[:, None] == jnp.arange(block_size, dtype=jnp.int32)[None, :]).astype(jnp.float32)
    return 0.5 * (unit_cols + sign_cols)

def cell_partial(operands):
    values, potential_cell = operands
    weighted = (values.astype(jnp.float32) * potential_cell[:, None]).astype(jnp.bfloat16)
    return lax.dot_general(weighted, values, (((0,), (0,)), ((), ())), preferred_element_type=jnp.float32)

def reference(basis_values, potential, block_lists):
    block_size = basis_values.shape[3] // 9
    cell_total = REGIONS * LINES
    partial_all = lax.map(cell_partial, (basis_values.reshape(cell_total, POINTS, 9 * block_size), potential.reshape(cell_total, POINTS)))
    partial_all = partial_all.reshape(REGIONS, LINES, 9, block_size, 9, block_size)
    codes_flat = block_lists.reshape(cell_total, MAXB)

    def one_cell(operands):
        index, slot_codes = operands
        region = index // LINES
        line_pos = index % LINES
        block_rows = []
        for first in range(MAXB):
            row_blocks = []
            for second in range(MAXB):
                code_first = slot_codes[first]
                code_second = slot_codes[second]
                first_a = code_first // 3 - 1
                first_r = code_first % 3 - 1
                second_a = code_second // 3 - 1
                second_r = code_second % 3 - 1
                total = jnp.zeros((block_size, block_size), jnp.float32)
                for shift_a in (-1, 0, 1):
                    for shift_r in (-1, 0, 1):
                        source_a = (region + first_a - shift_a) % REGIONS
                        source_r = line_pos + first_r - shift_r
                        rel_a = second_a - first_a + shift_a
                        rel_r = second_r - first_r + shift_r
                        usable = (code_first >= 0) & (code_second >= 0) & (source_r >= 0) & (source_r < LINES)
                        usable = usable & (jnp.abs(rel_a) <= 1) & (jnp.abs(rel_r) <= 1)
                        rel_code = jnp.clip((rel_a + 1) * 3 + rel_r + 1, 0, 8).astype(jnp.int32)
                        tile_block = partial_all[source_a, jnp.clip(source_r, 0, LINES - 1).astype(jnp.int32), (shift_a + 1) * 3 + shift_r + 1, :, rel_code, :]
                        total = total + jnp.where(usable, tile_block, jnp.float32(0.0))
                row_blocks.append(total)
            block_rows.append(jnp.concatenate(row_blocks, axis=1))
        submatrix = jnp.concatenate(block_rows, axis=0)
        live_blocks = jnp.sum((slot_codes >= 0).astype(jnp.int32))
        return newton_sign(submatrix, live_blocks, block_size)
    result = lax.map(one_cell, (jnp.arange(cell_total, dtype=jnp.int32), codes_flat))
    return result.reshape(REGIONS, LINES, MAXB * block_size, block_size)
```

```python
import functools

import jax
import jax.numpy as jnp
from jax import lax
from jax.experimental import pallas as pl
from jax.experimental.pallas import tpu as pltpu
from jax.sharding import PartitionSpec as P

F32 = jnp.float32
BF16 = jnp.bfloat16
REACH = 3


def ring(peers, wrap):
    up = [(i, (i + 1) % peers) for i in range(peers if wrap else peers - 1)]
    return up, [(j, i) for i, j in up]


def extended_2(shard, sides, width, wrap):
    for axis, dim in sides:
        peers, length = (lax.axis_size(axis), shard.shape[dim])
        up, down = ring(peers, wrap)
        last = lax.slice_in_dim(shard, length - width, length, axis=dim)
        first = lax.slice_in_dim(shard, 0, width, axis=dim)
        before = lax.ppermute(last, axis, up)
        after = lax.ppermute(first, axis, down)
        shard = jnp.concatenate([before, shard, after], axis=dim)
    return shard


def combine_three(below_part, centre_part, above_part, dim_index):

    def place(portion, before):
        widths = [(0, 0)] * portion.ndim
        widths[dim_index] = (before, 2 - before)
        return jnp.pad(portion, widths)

    return place(below_part, 0) + place(centre_part, 1) + place(above_part, 2)


def product_kernel(groups, lines, start_ref, values_ref, potential_ref, *refs):
    outs, (held, sems) = refs[:-2], refs[-2:]
    wide = held.shape[2]
    block = wide // lines
    start = start_ref[0]
    copies = []
    for a in range(REACH):
        columns = pl.ds(pl.multiple_of(a * REACH * block + start * block, block), wide)
        copy = pltpu.make_async_copy(values_ref.at[0, 0, :, columns], held.at[a], sems.at[a])
        copy.start()
        copies.append(copy)
    for copy in copies:
        copy.wait()
    level = potential_ref[0, :, :]
    for out, (row, columns) in zip(outs, groups):
        left = held[row].T
        left = (left.astype(F32) * level).astype(BF16)
        for i, column in enumerate(columns):
            out[:, i * wide : (i + 1) * wide] = jnp.dot(
                left, held[column], preferred_element_type=F32
            )


def local_products(values, potential, start, groups, lines):
    points, width = values.shape[2:]
    wide = width // (REACH * REACH) * lines
    flops = sum(2 * points * wide * wide * len(columns) for _, columns in groups)
    return pl.pallas_call(
        functools.partial(product_kernel, groups, lines),
        out_shape=[jax.ShapeDtypeStruct((wide, wide * len(c)), F32) for _, c in groups],
        in_specs=[
            pl.BlockSpec(memory_space=pltpu.SMEM),
            pl.BlockSpec(memory_space=pl.ANY),
            pl.BlockSpec(memory_space=pltpu.VMEM),
        ],
        out_specs=[pl.BlockSpec(memory_space=pltpu.VMEM) for _ in groups],
        scratch_shapes=[
            pltpu.VMEM((REACH, points, wide), BF16),
            pltpu.SemaphoreType.DMA((REACH,)),
        ],
        cost_estimate=pl.CostEstimate(
            flops=flops, bytes_accessed=2 * points * wide * REACH, transcendentals=0
        ),
        name="products",
    )(start, values, potential)


def sign_kernel(slots, block, place, meta_ref, *refs):
    pieces, (out_ref, sh, xf, xb, sb) = refs[:-5], refs[-5:]
    size = sh.shape[0]
    live_count = (meta_ref[0] * block).astype(F32)
    own = meta_ref[1]
    used = [meta_ref[2 + k].astype(F32) for k in range(slots)]
    eye = (
        lax.broadcasted_iota(jnp.int32, (block, block), 0)
        == lax.broadcasted_iota(jnp.int32, (block, block), 1)
    ).astype(F32)

    def read(k, l):
        total = None
        for piece, row, column in place(k, l):
            part = pieces[piece][
                row * block : (row + 1) * block, column * block : (column + 1) * block
            ]
            total = part if total is None else total + part
        return total

    trace = sum(jnp.sum(read(k, k) * eye) * used[k] for k in range(slots))
    mean_level = trace / live_count
    square_sum = jnp.zeros((block, block), F32)
    for k in range(slots):
        for l in range(slots):
            part = read(k, l)
            part = (mean_level * eye - part if k == l else -part) * (used[k] * used[l])
            square_sum = square_sum + part * part
            rows, columns = pl.ds(k * block, block), pl.ds(l * block, block)
            sh[rows, columns] = part
            xb[rows, columns] = part.astype(BF16)
    norm = lax.rsqrt(jnp.full((1, 1), jnp.sum(square_sum) + 1e-06, F32)) * jnp.sqrt(
        jnp.full((1, 1), live_count, F32)
    )
    dot = functools.partial(jnp.dot, preferred_element_type=F32)
    sb[...] = (dot(xb[...], xb[...]) * (norm * norm)).astype(BF16)
    fourth = dot(sb[...], sb[...])
    rho = jnp.sqrt(jnp.sqrt(jnp.sqrt(jnp.full((1, 1), jnp.sum(fourth * fourth) + 1e-06, F32))))
    inverse = 1.0 / rho
    first = norm * inverse
    xf[...] = (1.5 * first) * sh[...] - (0.5 * first * inverse * inverse) * dot(xb[...], sb[...])
    xb[...] = xf[...].astype(BF16)
    sb[...] = dot(xb[...], xb[...]).astype(BF16)
    xf[...] = 1.5 * xf[...] - 0.5 * dot(xb[...], sb[...])
    xb[...] = xf[...].astype(BF16)

    columns = xf[:, pl.ds(pl.multiple_of(own * block, block), block)]

    def thin(v):
        high = v.astype(BF16)
        low = (v - high.astype(F32)).astype(BF16)
        both = dot(xb[...], jnp.concatenate([high, low], axis=1))
        return both[:, :block] + both[:, block:]

    sh[:, :block] = 1.5 * columns - 0.5 * thin(thin(columns))
    for s in range(slots):
        source = meta_ref[2 + slots + s]
        rows = sh[pl.ds(pl.multiple_of(jnp.maximum(source, 0) * block, block), block), :block]
        rows = jnp.where(source >= 0, rows, 0.0)
        out_ref[s * block : (s + 1) * block, :] = 0.5 * (rows + eye if s == 0 else rows)


def sign_columns(meta, pieces, place, slots, block):
    size = slots * block
    vmem = pl.BlockSpec(memory_space=pltpu.VMEM)
    return pl.pallas_call(
        functools.partial(sign_kernel, slots, block, place),
        out_shape=jax.ShapeDtypeStruct((size, block), F32),
        in_specs=[pl.BlockSpec(memory_space=pltpu.SMEM)] + [vmem] * len(pieces),
        out_specs=vmem,
        scratch_shapes=[
            pltpu.VMEM((size, size), F32),
            pltpu.VMEM((size, size), F32),
            pltpu.VMEM((size, size), BF16),
            pltpu.VMEM((size, size), BF16),
        ],
        cost_estimate=pl.CostEstimate(
            flops=12 * size**3, bytes_accessed=4 * size * size, transcendentals=0
        ),
        name="sign",
    )(meta, *pieces)


def shards_dense_line(basis_values, potential, block_lists):
    codes = block_lists[0, 0]
    lines = lax.axis_size("grid")
    position = lax.axis_index("grid")
    width = basis_values.shape[3]
    block = width // (REACH * REACH)
    wide = lines * block
    slots = REACH * lines
    up, down = ring(lax.axis_size("atoms"), True)
    line_shifts = [[(i, (i + s) % lines) for i in range(lines)] for s in range(1, lines)]
    start = (1 - position).astype(jnp.int32)[None]

    def line_sum(part):
        return part + sum(lax.ppermute(part, "grid", shift) for shift in line_shifts)

    low, high = local_products(
        basis_values, potential, start, ((0, (0, 1, 2)), (2, (0, 1, 2))), lines
    )
    from_low = lax.ppermute(high[:, wide:], "atoms", up)
    from_high = lax.ppermute(low[:, : 2 * wide], "atoms", down)
    corners = line_sum(jnp.concatenate([low[:, 2 * wide :], high[:, :wide]], axis=0))
    (middle,) = local_products(basis_values, potential, start, ((1, (0, 1, 2)),), lines)
    own = (
        middle
        + jnp.pad(from_low, ((0, 0), (0, wide)))
        + jnp.pad(from_high, ((0, 0), (wide, 0)))
    )
    own = line_sum(own)
    below = lax.ppermute(own[:, wide:], "atoms", up)
    above = lax.ppermute(own[:, : 2 * wide], "atoms", down)

    def place(k, l):
        a, row = divmod(k, lines)
        b, column = divmod(l, lines)
        if a == 1:
            return [(0, row, b * lines + column)]
        if a == 0:
            return [(1, row, b * lines + column)] if b < 2 else [(3, row, column)]
        return [(2, row, (b - 1) * lines + column)] if b > 0 else [(3, lines + row, column)]

    live = jnp.sum((codes >= 0).astype(jnp.int32))
    source = (codes // REACH) * lines + codes % REACH - 1 + position
    source = jnp.where(codes >= 0, source, -1).astype(jnp.int32)
    blocks = jnp.arange(slots, dtype=jnp.int32)
    used = jnp.sum((source[None, :] == blocks[:, None]).astype(jnp.int32), axis=1)
    meta = jnp.concatenate([live[None], (lines + position)[None].astype(jnp.int32), used, source])
    return sign_columns(meta, (own, below, above, corners), place, slots, block)[None, None]


def shards(basis_values, potential, block_lists):
    values = basis_values[0, 0]
    potential_cell = potential[0, 0]
    slot_codes = block_lists[0, 0]
    slots = slot_codes.shape[0]
    block_size = values.shape[1] // 9
    weighted = (values.astype(jnp.float32) * potential_cell[:, None]).astype(jnp.bfloat16)
    partial_sums = lax.dot_general(
        weighted, values, (((0,), (0,)), ((), ())), preferred_element_type=jnp.float32
    )
    partial_tiles = partial_sums.reshape(3, 3, block_size, 3, 3, block_size)
    extended = extended_2(partial_tiles, (("atoms", 0),), 1, True)
    middle = combine_three(extended[0], extended[2], extended[4], 2)
    extended_line = extended_2(middle, (("grid", 0),), 1, False)
    own_rows = combine_three(extended_line[0], extended_line[2], extended_line[4], 2)
    packed = jnp.stack([own_rows[:, 0:3], own_rows[:, 2:5]])
    arrived = extended_2(packed, (("atoms", 0),), 1, True)
    nearby = jnp.stack([arrived[0], own_rows[:, 1:4], arrived[3]])
    packed_line = jnp.stack([nearby[:, :, :, 0:3], nearby[:, :, :, 2:5]])
    arrived_line = extended_2(packed_line, (("grid", 0),), 1, False)
    gathered = jnp.stack([arrived_line[0], nearby[:, :, :, 1:4], arrived_line[3]], axis=1)
    block_grid = gathered.reshape(9, block_size, 9, block_size)
    selector = (slot_codes[:, None] == jnp.arange(9, dtype=jnp.int32)[None, :]).astype(jnp.float32)
    picked_rows = jnp.einsum("sk,kimj->simj", selector, block_grid, precision=lax.Precision.HIGHEST)
    submatrix = jnp.einsum("simj,tm->sitj", picked_rows, selector, precision=lax.Precision.HIGHEST)
    submatrix = submatrix.reshape(slots * block_size, slots * block_size)
    used = (slot_codes >= 0).astype(jnp.int32)
    source = jnp.where(slot_codes >= 0, jnp.arange(slots, dtype=jnp.int32), -1)
    meta = jnp.concatenate([jnp.sum(used)[None], jnp.zeros((1,), jnp.int32), used, source])
    return sign_columns(
        meta, (submatrix,), lambda k, l: [(0, k, l)], slots, block_size
    )[None, None]


def solution(mesh):
    placed = (P("atoms", "grid", None, None), P("atoms", "grid", None), P("atoms", "grid", None))
    dense = mesh.shape["grid"] == 2 and mesh.shape["atoms"] >= 5

    def body(basis_values, potential, block_lists):
        slots = block_lists.shape[2]
        if dense and slots == REACH * mesh.shape["grid"]:
            return shards_dense_line(basis_values, potential, block_lists)
        return shards(basis_values, potential, block_lists)

    return jax.shard_map(
        body,
        mesh=mesh,
        in_specs=placed,
        out_specs=P("atoms", "grid", None, None),
        check_vma=False,
    )
```

```python
import functools

import jax
import jax.numpy as jnp
from jax import lax
from jax.experimental import pallas as pl
from jax.experimental.pallas import tpu as pltpu
from jax.sharding import PartitionSpec as P

F32 = jnp.float32
BF16 = jnp.bfloat16
REACH = 3
KERNEL_BYTES = 32 * 1024 * 1024
LOADING_BYTES = 50 * 1024 * 1024


def ring(peers, wrap):
    up = [(i, (i + 1) % peers) for i in range(peers if wrap else peers - 1)]
    return up, [(j, i) for i, j in up]


def extended_2(shard, sides, width, wrap):
    for axis, dim in sides:
        peers, length = (lax.axis_size(axis), shard.shape[dim])
        up, down = ring(peers, wrap)
        last = lax.slice_in_dim(shard, length - width, length, axis=dim)
        first = lax.slice_in_dim(shard, 0, width, axis=dim)
        before = lax.ppermute(last, axis, up)
        after = lax.ppermute(first, axis, down)
        shard = jnp.concatenate([before, shard, after], axis=dim)
    return shard


def combine_three(below_part, centre_part, above_part, dim_index):

    def place(portion, before):
        widths = [(0, 0)] * portion.ndim
        widths[dim_index] = (before, 2 - before)
        return jnp.pad(portion, widths)

    return place(below_part, 0) + place(centre_part, 1) + place(above_part, 2)


def product_kernel(outputs, lines, chunks, start_ref, values_ref, potential_ref, *refs):
    outs, (held, turned, total, sems) = refs[:-4], refs[-4:]
    depth, size = held.shape[1:]
    wide = size // REACH
    block = wide // lines
    start = start_ref[0]
    copies = []
    for c in range(chunks):
        for a in range(REACH):
            columns = pl.ds(pl.multiple_of(a * REACH * block + start * block, block), wide)
            copies.append(
                pltpu.make_async_copy(
                    values_ref.at[0, 0, pl.ds(c * depth, depth), columns],
                    held.at[c, :, pl.ds(a * wide, wide)],
                    sems.at[c, a],
                )
            )
            copies[-1].start()

    def prepare(c):
        for a in range(REACH):
            copies[c * REACH + a].wait()
        level = potential_ref[0, :, c * depth : (c + 1) * depth]
        turned[c % 2] = (held[c].T.astype(F32) * level).astype(BF16)

    prepare(0)
    for c in range(chunks):
        if c + 1 < chunks:
            prepare(c + 1)
        for a in range(REACH):
            columns = pl.ds(a * wide, wide)
            part = jnp.dot(turned[c % 2], held[c, :, columns], preferred_element_type=F32)
            total[:, columns] = part if c == 0 else total[:, columns] + part

    def mean(i, j):
        rows, columns = pl.ds(i * block, block), pl.ds(j * block, block)
        return 0.5 * (total[rows, columns] + total[columns, rows].T)

    for out, pairs in zip(outs, outputs):
        for n, (i, j) in enumerate(pairs):
            out[n * block : (n + 1) * block, :] = mean(i, j)


def local_products(values, potential, start, outputs, lines):
    points, width = values.shape[2:]
    block = width // (REACH * REACH)
    size = block * lines * REACH
    chunks = 4
    vmem = pl.BlockSpec(memory_space=pltpu.VMEM)
    return pl.pallas_call(
        functools.partial(product_kernel, outputs, lines, chunks),
        out_shape=[jax.ShapeDtypeStruct((len(pairs) * block, block), F32) for pairs in outputs],
        in_specs=[
            pl.BlockSpec(memory_space=pltpu.SMEM),
            pl.BlockSpec(memory_space=pltpu.HBM),
            vmem,
        ],
        out_specs=[vmem] * len(outputs),
        scratch_shapes=[
            pltpu.VMEM((chunks, points // chunks, size), BF16),
            pltpu.VMEM((2, size, points // chunks), BF16),
            pltpu.VMEM((size, size), F32),
            pltpu.SemaphoreType.DMA((chunks, REACH)),
        ],
        compiler_params=pltpu.CompilerParams(vmem_limit_bytes=LOADING_BYTES),
        cost_estimate=pl.CostEstimate(
            flops=2 * points * size * size, bytes_accessed=2 * points * size, transcendentals=0
        ),
        name="products",
    )(start, values, potential)


def sign_kernel(slots, block, own_tile, place, meta_ref, *refs):
    pieces, (out_ref, xf, cf, yf, xb, sb, yb) = refs[:-7], refs[-7:]
    size, tile = yf.shape
    tiles, per_tile = size // tile, tile // block
    live_count = (meta_ref[0] * block).astype(F32)
    used = [meta_ref[2 + k].astype(F32) for k in range(slots)]
    eye = (
        lax.broadcasted_iota(jnp.int32, (block, block), 0)
        == lax.broadcasted_iota(jnp.int32, (block, block), 1)
    ).astype(F32)
    dot = functools.partial(jnp.dot, preferred_element_type=F32)

    def at(i, width=tile):
        return pl.ds(i * width, width)

    def read(k, l):
        total = None
        for piece, n in place(k, l):
            part = pieces[piece][n * block : (n + 1) * block, :]
            total = part if total is None else total + part
        return total

    def fold(x):
        return jnp.sum(x.reshape(x.shape[0] // 8, 8, x.shape[1]), axis=0)

    def columns_of(left, right):
        for j in range(tiles):
            yield j, dot(left[: (j + 1) * tile, :], right[:, at(j)])

    def keep(to, j, upper):
        upper = upper.astype(BF16)
        to[: (j + 1) * tile, at(j)] = upper
        for i in range(j):
            to[at(j), at(i)] = upper[i * tile : (i + 1) * tile].T

    trace = sum(jnp.sum(read(k, k) * eye) * used[k] for k in range(slots))
    mean_level = trace / live_count
    square_sum = jnp.zeros((8, block), F32)
    for k in range(slots):
        for l in range(k, slots):
            part = read(k, l)
            part = (mean_level * eye - part if k == l else -part) * (used[k] * used[l])
            square_sum = square_sum + fold(part * part) * (1.0 if k == l else 2.0)
            rows, columns = at(k, block), at(l, block)
            xf[rows, columns] = part
            xb[rows, columns] = part.astype(BF16)
            if k < l:
                mirror = part.T
                xb[columns, rows] = mirror.astype(BF16)
                if k // per_tile == l // per_tile:
                    xf[columns, rows] = mirror
    norm = lax.rsqrt(jnp.full((1, 1), jnp.sum(square_sum) + 1e-06, F32)) * jnp.sqrt(
        jnp.full((1, 1), live_count, F32)
    )
    for j, square in columns_of(xb, xb):
        keep(sb, j, square * (norm * norm))
    fourth_sum = jnp.zeros((8, tile), F32)
    for j, fourth in columns_of(sb, sb):
        fourth = fourth * fourth
        fourth_sum = fourth_sum + fold(fourth[j * tile :])
        if j:
            fourth_sum = fourth_sum + 2.0 * fold(fourth[: j * tile])
    for j, cube in columns_of(xb, sb):
        cf[: (j + 1) * tile, at(j)] = cube
    rho = jnp.sqrt(jnp.sqrt(jnp.sqrt(jnp.full((1, 1), jnp.sum(fourth_sum) + 1e-06, F32))))
    inverse = 1.0 / rho
    first = norm * inverse
    for j in range(tiles):
        rows, columns = pl.ds(0, (j + 1) * tile), at(j)
        upper = (1.5 * first) * xf[rows, columns] - (0.5 * first * inverse * inverse) * cf[
            rows, columns
        ]
        xf[rows, columns] = upper
        keep(xb, j, upper)
    for j, square in columns_of(xb, xb):
        keep(sb, j, square)
    for j, cube in columns_of(xb, sb):
        upper = 1.5 * xf[: (j + 1) * tile, at(j)] - 0.5 * cube
        keep(yb, j, upper)
        if j == own_tile:
            yf[: (j + 1) * tile, :] = upper
        elif j > own_tile:
            yf[at(j), :] = upper[own_tile * tile : (own_tile + 1) * tile].T

    columns = yf[:, pl.ds(pl.multiple_of(meta_ref[1] * block, block), block)]

    def thin(v):
        high = v.astype(BF16)
        low = (v - high.astype(F32)).astype(BF16)
        both = dot(yb[...], jnp.concatenate([high, low], axis=1))
        return both[:, :block] + both[:, block:]

    xf[:, :block] = 1.5 * columns - 0.5 * thin(thin(columns))
    for s in range(slots):
        source = meta_ref[2 + slots + s]
        rows = xf[pl.ds(pl.multiple_of(jnp.maximum(source, 0) * block, block), block), :block]
        rows = jnp.where(source >= 0, rows, 0.0)
        out_ref[s * block : (s + 1) * block, :] = 0.5 * (rows + eye if s == 0 else rows)


def sign_columns(meta, pieces, place, slots, block, own_tile):
    size = slots * block
    tile = block * (2 if slots % 2 == 0 else 1)
    vmem = pl.BlockSpec(memory_space=pltpu.VMEM)
    return pl.pallas_call(
        functools.partial(sign_kernel, slots, block, own_tile, place),
        out_shape=jax.ShapeDtypeStruct((size, block), F32),
        in_specs=[pl.BlockSpec(memory_space=pltpu.SMEM)] + [vmem] * len(pieces),
        out_specs=vmem,
        scratch_shapes=[
            pltpu.VMEM((size, size), F32),
            pltpu.VMEM((size, size), F32),
            pltpu.VMEM((size, tile), F32),
            pltpu.VMEM((size, size), BF16),
            pltpu.VMEM((size, size), BF16),
            pltpu.VMEM((size, size), BF16),
        ],
        compiler_params=pltpu.CompilerParams(vmem_limit_bytes=KERNEL_BYTES),
        cost_estimate=pl.CostEstimate(
            flops=8 * size**3, bytes_accessed=4 * size * size, transcendentals=0
        ),
        name="sign",
    )(meta, *pieces)


def shards_dense_line(basis_values, potential, block_lists):
    codes = block_lists[0, 0]
    lines = lax.axis_size("grid")
    position = lax.axis_index("grid")
    block = basis_values.shape[3] // (REACH * REACH)
    slots = REACH * lines
    up, down = ring(lax.axis_size("atoms"), True)
    line_shifts = [[(i, (i + s) % lines) for i in range(lines)] for s in range(1, lines)]
    start = (1 - position).astype(jnp.int32)[None]

    def line_parts(part):
        return [lax.ppermute(part, "grid", shift) for shift in line_shifts]

    half = lines // 2
    triangle = [(r, q) for r in range(lines) for q in range(r, lines)]

    def within(a):
        return [(a * lines + r, a * lines + q) for r, q in triangle]

    def across(a, b, rows):
        return [(a * lines + r, b * lines + q) for r in rows for q in range(lines)]

    early, late = range(half), range(half, lines)
    up_own, up_side, down_own, down_side, outer, own, side = local_products(
        basis_values,
        potential,
        start,
        (
            within(2),
            across(1, 2, early),
            within(0),
            across(0, 1, late),
            across(0, 2, range(lines)),
            within(1),
            across(0, 1, early) + across(1, 2, late),
        ),
        lines,
    )
    outer_parts = [outer] + line_parts(outer)
    own = own + lax.ppermute(up_own, "atoms", up) + lax.ppermute(down_own, "atoms", down)
    up_side, down_side = lax.ppermute(up_side, "atoms", up), lax.ppermute(down_side, "atoms", down)
    side = side + jnp.concatenate([up_side, down_side])
    own = sum(line_parts(own), own)
    side = sum(line_parts(side), side)
    below_own = lax.ppermute(own, "atoms", up)
    above_own = lax.ppermute(own, "atoms", down)
    cut = half * lines * block
    below_side = lax.ppermute(side[cut:], "atoms", up)
    above_side = lax.ppermute(side[:cut], "atoms", down)
    pieces = [own, side, below_own, above_own, below_side, above_side] + outer_parts

    def place(k, l):
        (a, r), (b, q) = divmod(k, lines), divmod(l, lines)
        if a == b:
            return [((2, 0, 3)[a], triangle.index((r, q)))]
        if b - a == 2:
            return [(n, r * lines + q) for n in range(6, len(pieces))]
        if r < half:
            return [((1, 5)[a], r * lines + q)]
        if a == 0:
            return [(4, (r - half) * lines + q)]
        return [(1, r * lines + q)]

    live = jnp.sum((codes >= 0).astype(jnp.int32))
    source = (codes // REACH) * lines + codes % REACH - 1 + position
    source = jnp.where(codes >= 0, source, -1).astype(jnp.int32)
    blocks = jnp.arange(slots, dtype=jnp.int32)
    used = jnp.sum((source[None, :] == blocks[:, None]).astype(jnp.int32), axis=1)
    meta = jnp.concatenate([live[None], position[None].astype(jnp.int32), used, source])
    return sign_columns(meta, pieces, place, slots, block, 1)[None, None]


def shards(basis_values, potential, block_lists):
    values = basis_values[0, 0]
    potential_cell = potential[0, 0]
    slot_codes = block_lists[0, 0]
    slots = slot_codes.shape[0]
    block_size = values.shape[1] // 9
    weighted = (values.astype(jnp.float32) * potential_cell[:, None]).astype(jnp.bfloat16)
    partial_sums = lax.dot_general(
        weighted, values, (((0,), (0,)), ((), ())), preferred_element_type=jnp.float32
    )
    partial_sums = 0.5 * (partial_sums + partial_sums.T)
    partial_tiles = partial_sums.reshape(3, 3, block_size, 3, 3, block_size)
    extended = extended_2(partial_tiles, (("atoms", 0),), 1, True)
    middle = combine_three(extended[0], extended[2], extended[4], 2)
    extended_line = extended_2(middle, (("grid", 0),), 1, False)
    own_rows = combine_three(extended_line[0], extended_line[2], extended_line[4], 2)
    packed = jnp.stack([own_rows[:, 0:3], own_rows[:, 2:5]])
    arrived = extended_2(packed, (("atoms", 0),), 1, True)
    nearby = jnp.stack([arrived[0], own_rows[:, 1:4], arrived[3]])
    packed_line = jnp.stack([nearby[:, :, :, 0:3], nearby[:, :, :, 2:5]])
    arrived_line = extended_2(packed_line, (("grid", 0),), 1, False)
    gathered = jnp.stack([arrived_line[0], nearby[:, :, :, 1:4], arrived_line[3]], axis=1)
    block_grid = gathered.reshape(9, block_size, 9, block_size)
    selector = (slot_codes[:, None] == jnp.arange(9, dtype=jnp.int32)[None, :]).astype(jnp.float32)
    picked_rows = jnp.einsum("sk,kimj->simj", selector, block_grid, precision=lax.Precision.HIGHEST)
    submatrix = jnp.einsum("simj,tm->sitj", picked_rows, selector, precision=lax.Precision.HIGHEST)
    pieces = [submatrix[k, :, k:].transpose(1, 0, 2).reshape(-1, block_size) for k in range(slots)]
    used = (slot_codes >= 0).astype(jnp.int32)
    source = jnp.where(slot_codes >= 0, jnp.arange(slots, dtype=jnp.int32), -1)
    meta = jnp.concatenate([jnp.sum(used)[None], jnp.zeros((1,), jnp.int32), used, source])
    return sign_columns(meta, pieces, lambda k, l: [(k, l - k)], slots, block_size, 0)[None, None]


def solution(mesh):
    placed = (P("atoms", "grid", None, None), P("atoms", "grid", None), P("atoms", "grid", None))
    dense = mesh.shape["grid"] == 2 and mesh.shape["atoms"] >= 5

    def body(basis_values, potential, block_lists):
        if dense and block_lists.shape[2] == REACH * mesh.shape["grid"]:
            return shards_dense_line(basis_values, potential, block_lists)
        return shards(basis_values, potential, block_lists)

    return jax.shard_map(
        body,
        mesh=mesh,
        in_specs=placed,
        out_specs=P("atoms", "grid", None, None),
        check_vma=False,
    )
```

```python
import functools

import jax
import jax.numpy as jnp
from jax import lax
from jax.experimental import pallas as pl
from jax.experimental.pallas import tpu as pltpu
from jax.sharding import PartitionSpec as P

F32 = jnp.float32
BF16 = jnp.bfloat16
REACH = 3
KERNEL_BYTES = 32 * 1024 * 1024
LOADING_BYTES = 50 * 1024 * 1024


def ring(peers, wrap):
    up = [(i, (i + 1) % peers) for i in range(peers if wrap else peers - 1)]
    return up, [(j, i) for i, j in up]


def extended_2(shard, sides, width, wrap):
    for axis, dim in sides:
        peers, length = (lax.axis_size(axis), shard.shape[dim])
        up, down = ring(peers, wrap)
        last = lax.slice_in_dim(shard, length - width, length, axis=dim)
        first = lax.slice_in_dim(shard, 0, width, axis=dim)
        before = lax.ppermute(last, axis, up)
        after = lax.ppermute(first, axis, down)
        shard = jnp.concatenate([before, shard, after], axis=dim)
    return shard


def combine_three(below_part, centre_part, above_part, dim_index):

    def place(portion, before):
        widths = [(0, 0)] * portion.ndim
        widths[dim_index] = (before, 2 - before)
        return jnp.pad(portion, widths)

    return place(below_part, 0) + place(centre_part, 1) + place(above_part, 2)


def product_kernel(both_pairs, lines, chunks, start_ref, values_ref, potential_ref, *refs):
    outs, (held, turned, total, means, levels, sems, level_sem) = refs[:-7], refs[-7:]
    depth, size = held.shape[1:]
    wide = size // REACH
    block = wide // lines
    start = start_ref[0]
    level_copy = pltpu.make_async_copy(potential_ref.at[0], levels, level_sem)
    level_copy.start()
    copies = []
    for c in range(chunks):
        for a in range(REACH):
            columns = pl.ds(pl.multiple_of(a * REACH * block + start * block, block), wide)
            copies.append(
                pltpu.make_async_copy(
                    values_ref.at[0, 0, pl.ds(c * depth, depth), columns],
                    held.at[c, :, pl.ds(a * wide, wide)],
                    sems.at[c, a],
                )
            )
            copies[-1].start()

    def prepare(c):
        for a in range(REACH):
            copies[c * REACH + a].wait()
        level = levels[:, c * depth : (c + 1) * depth]
        turned[c % 2] = (held[c].T.astype(F32) * level).astype(BF16)

    level_copy.wait()
    prepare(0)
    for c in range(chunks):
        if c + 1 < chunks:
            prepare(c + 1)
        for n in range(0, size, 256):
            for m in range(0, size, 768):
                here = pl.ds(m, 768), pl.ds(n, 256)
                part = jnp.dot(
                    turned[c % 2, here[0], :], held[c, :, here[1]], preferred_element_type=F32
                )
                total[here] = part if c == 0 else total[here] + part

    wanted = sorted({pair for lists in both_pairs for pairs in lists for pair in pairs})
    for n, (i, j) in enumerate(wanted):
        rows, columns = pl.ds(i * block, block), pl.ds(j * block, block)
        means[n] = 0.5 * (total[rows, columns] + total[columns, rows].T)
    odd = start_ref[1] == 1
    for out, evens, odds in zip(outs, *both_pairs):
        for n, (even_pair, odd_pair) in enumerate(zip(evens, odds)):
            index = wanted.index(even_pair)
            if even_pair != odd_pair:
                index = jnp.where(odd, wanted.index(odd_pair), index)
            out[n * block : (n + 1) * block, :] = means[index]


def local_products(values, potential, start, both_pairs, lines):
    points, width = values.shape[2:]
    block = width // (REACH * REACH)
    size = block * lines * REACH
    chunks = 1
    vmem = pl.BlockSpec(memory_space=pltpu.VMEM)
    counts = [len(pairs) for pairs in both_pairs[0]]
    return pl.pallas_call(
        functools.partial(product_kernel, both_pairs, lines, chunks),
        out_shape=[jax.ShapeDtypeStruct((n * block, block), F32) for n in counts],
        in_specs=[
            pl.BlockSpec(memory_space=pltpu.SMEM),
            pl.BlockSpec(memory_space=pltpu.HBM),
            pl.BlockSpec(memory_space=pltpu.HBM),
        ],
        out_specs=[vmem] * len(counts),
        scratch_shapes=[
            pltpu.VMEM((chunks, points // chunks, size), BF16),
            pltpu.VMEM((2, size, points // chunks), BF16),
            pltpu.VMEM((size, size), F32),
            pltpu.VMEM((REACH * REACH * lines * lines, block, block), F32),
            pltpu.VMEM((1, points), F32),
            pltpu.SemaphoreType.DMA((chunks, REACH)),
            pltpu.SemaphoreType.DMA,
        ],
        compiler_params=pltpu.CompilerParams(vmem_limit_bytes=LOADING_BYTES),
        cost_estimate=pl.CostEstimate(
            flops=2 * points * size * size, bytes_accessed=2 * points * size, transcendentals=0
        ),
        name="products",
    )(start, values, potential)


def sign_kernel(slots, block, own_tile, place, meta_ref, *refs):
    pieces, (out_ref, xf, cf, yf, xb, sb, yb) = refs[:-7], refs[-7:]
    size, tile = yf.shape
    tiles, per_tile = size // tile, tile // block
    live_count = (meta_ref[0] * block).astype(F32)
    used = [meta_ref[2 + k].astype(F32) for k in range(slots)]
    eye = (
        lax.broadcasted_iota(jnp.int32, (block, block), 0)
        == lax.broadcasted_iota(jnp.int32, (block, block), 1)
    ).astype(F32)
    dot = functools.partial(jnp.dot, preferred_element_type=F32)
    odd = meta_ref[2 + 2 * slots] == 1

    def at(i, width=tile):
        return pl.ds(i * width, width)

    def read(k, l):
        total = None
        for choices in place(k, l):
            parts = [pieces[piece][n * block : (n + 1) * block, :] for piece, n in choices]
            part = parts[0] if len(parts) == 1 else jnp.where(odd, parts[1], parts[0])
            total = part if total is None else total + part
        return total

    def fold(x):
        return jnp.sum(x.reshape(x.shape[0] // 8, 8, x.shape[1]), axis=0)

    def columns_of(left, right):
        for j in range(tiles):
            yield j, dot(left[: (j + 1) * tile, :], right[:, at(j)])

    def keep(to, j, upper):
        upper = upper.astype(BF16)
        to[: (j + 1) * tile, at(j)] = upper
        for i in range(j):
            to[at(j), at(i)] = upper[i * tile : (i + 1) * tile].T

    trace = jnp.sum(sum(fold(read(k, k) * eye) * used[k] for k in range(slots)))
    mean_level = trace / live_count
    square_sum = jnp.zeros((8, block), F32)
    for k in range(slots):
        for l in range(k, slots):
            part = read(k, l)
            if k == l:
                part = part - mean_level * eye
            part = part * -(used[k] * used[l])
            square_sum = square_sum + fold(part * part) * (1.0 if k == l else 2.0)
            rows, columns = at(k, block), at(l, block)
            xf[rows, columns] = part
            short = part.astype(BF16)
            xb[rows, columns] = short
            if k < l:
                xb[columns, rows] = short.T
                if k // per_tile == l // per_tile:
                    xf[columns, rows] = part.T
    norm = lax.rsqrt(jnp.full((1, 1), jnp.sum(square_sum) + 1e-06, F32)) * jnp.sqrt(
        jnp.full((1, 1), live_count, F32)
    )
    for j, square in columns_of(xb, xb):
        keep(sb, j, square * (norm * norm))
    fourth_sum = jnp.zeros((8, tile), F32)
    for j, fourth in columns_of(sb, sb):
        fourth = fourth * fourth
        fourth_sum = fourth_sum + fold(fourth[j * tile :])
        if j:
            fourth_sum = fourth_sum + 2.0 * fold(fourth[: j * tile])
    for j, cube in columns_of(xb, sb):
        cf[: (j + 1) * tile, at(j)] = cube
    rho = jnp.sqrt(jnp.sqrt(jnp.sqrt(jnp.full((1, 1), jnp.sum(fourth_sum) + 1e-06, F32))))
    inverse = 1.0 / rho
    first = norm * inverse
    for j in range(tiles):
        rows, columns = pl.ds(0, (j + 1) * tile), at(j)
        upper = (1.5 * first) * xf[rows, columns] - (0.5 * first * inverse * inverse) * cf[
            rows, columns
        ]
        xf[rows, columns] = upper
        keep(xb, j, upper)
    for j, square in columns_of(xb, xb):
        keep(sb, j, square)
    for j, cube in columns_of(xb, sb):
        upper = 1.5 * xf[: (j + 1) * tile, at(j)] - 0.5 * cube
        keep(yb, j, upper)
        if j == own_tile:
            yf[: (j + 1) * tile, :] = upper
        elif j > own_tile:
            yf[at(j), :] = upper[own_tile * tile : (own_tile + 1) * tile].T

    columns = yf[:, pl.ds(pl.multiple_of(meta_ref[1] * block, block), block)]

    def thin(v):
        high = v.astype(BF16)
        low = (v - high.astype(F32)).astype(BF16)
        halves = []
        for n, pair in enumerate(((high, low), (low, high))):
            rows = pl.ds(n * size // 2, size // 2)
            both = dot(yb[rows, :], jnp.concatenate(pair, axis=1))
            halves.append(both[:, :block] + both[:, block:])
        return jnp.concatenate(halves, axis=0)

    xf[:, :block] = 1.5 * columns - 0.5 * thin(thin(columns))
    for s in range(slots):
        source = meta_ref[2 + slots + s]
        rows = xf[pl.ds(pl.multiple_of(jnp.maximum(source, 0) * block, block), block), :block]
        rows = jnp.where(source >= 0, rows, 0.0)
        out_ref[s * block : (s + 1) * block, :] = 0.5 * (rows + eye if s == 0 else rows)


def sign_columns(meta, pieces, place, slots, block, own_tile):
    size = slots * block
    tile = block * (2 if slots % 2 == 0 else 1)
    vmem = pl.BlockSpec(memory_space=pltpu.VMEM)
    return pl.pallas_call(
        functools.partial(sign_kernel, slots, block, own_tile, place),
        out_shape=jax.ShapeDtypeStruct((size, block), F32),
        in_specs=[pl.BlockSpec(memory_space=pltpu.SMEM)] + [vmem] * len(pieces),
        out_specs=vmem,
        scratch_shapes=[
            pltpu.VMEM((size, size), F32),
            pltpu.VMEM((size, size), F32),
            pltpu.VMEM((size, tile), F32),
            pltpu.VMEM((size, size), BF16),
            pltpu.VMEM((size, size), BF16),
            pltpu.VMEM((size, size), BF16),
        ],
        compiler_params=pltpu.CompilerParams(vmem_limit_bytes=KERNEL_BYTES),
        cost_estimate=pl.CostEstimate(
            flops=8 * size**3, bytes_accessed=4 * size * size, transcendentals=0
        ),
        name="sign",
    )(meta, *pieces)


def shards_dense_line(basis_values, potential, block_lists):
    codes = block_lists[0, 0]
    lines = lax.axis_size("grid")
    position = lax.axis_index("grid").astype(jnp.int32)
    parity = (lax.axis_index("atoms") % 2).astype(jnp.int32)
    block = basis_values.shape[3] // (REACH * REACH)
    slots = REACH * lines
    regions = lax.axis_size("atoms")
    far = [(i, (i + 1 if i % 2 else i - 1) % regions) for i in range(regions)]
    near = [(i, i - 1 if i % 2 else i + 1) for i in range(regions)]
    line_shifts = [[(i, (i + s) % lines) for i in range(lines)] for s in range(1, lines)]
    start = jnp.stack([1 - position, parity])

    def sent(part, axis, pairs):
        return lax.ppermute(part, axis, pairs)

    def line_parts(part):
        return [sent(part, "grid", shift) for shift in line_shifts]

    half = lines // 2
    triangle = [(r, q) for r in range(lines) for q in range(r, lines)]
    strip = [(r, q) for r in range(half) for q in range(lines)]

    def within(a):
        return [(a * lines + r, a * lines + q) for r, q in triangle]

    def across(a, late):
        first = half if late else 0
        return [(a * lines + first + r, (a + 1) * lines + q) for r, q in strip]

    def pairs_of(odd):
        return (
            within(2 * odd),
            within(2 - 2 * odd),
            across(odd, not odd),
            across(1 - odd, odd),
            within(1),
            across(odd, odd) + across(1 - odd, not odd),
            [(r, 2 * lines + q) for r in range(lines) for q in range(lines)],
        )

    own_to_far, own_to_near, side_to_far, side_to_near, own, side, outer = local_products(
        basis_values, potential, start, (pairs_of(0), pairs_of(1)), lines
    )
    outer_parts = [outer] + line_parts(outer)
    own = own + sent(own_to_far, "atoms", far) + sent(own_to_near, "atoms", near)
    side_far, side_near = sent(side_to_far, "atoms", far), sent(side_to_near, "atoms", near)
    side = side + jnp.concatenate([side_far, side_near])
    own = sum(line_parts(own), own)
    side = sum(line_parts(side), side)
    own_far = sent(own, "atoms", far)
    own_near = sent(own, "atoms", near)
    cut = len(strip) * block
    side_far = sent(side[:cut], "atoms", far)
    side_near = sent(side[cut:], "atoms", near)
    pieces = [own, own_far, own_near, side, side_far, side_near] + outer_parts

    def place(k, l):
        (a, r), (b, q) = divmod(k, lines), divmod(l, lines)
        if a == b:
            n = triangle.index((r, q))
            return [(((1, n), (2, n)), ((0, n),), ((2, n), (1, n)))[a]]
        if b - a == 2:
            return [((piece, r * lines + q),) for piece in range(6, len(pieces))]
        n = strip.index((r % half, q))
        kept, given = ((3, n), (3, len(strip) + n)), ((4, n), (5, n))
        choices = kept if (r < half) == (a == 0) else given
        return [choices if a == 0 else choices[::-1]]

    live = jnp.sum((codes >= 0).astype(jnp.int32))
    source = (codes // REACH) * lines + codes % REACH - 1 + position
    source = jnp.where(codes >= 0, source, -1).astype(jnp.int32)
    blocks = jnp.arange(slots, dtype=jnp.int32)
    used = jnp.sum((source[None, :] == blocks[:, None]).astype(jnp.int32), axis=1)
    meta = jnp.concatenate([live[None], position[None], used, source, parity[None]])
    return sign_columns(meta, pieces, place, slots, block, 1)[None, None]


def shards(basis_values, potential, block_lists):
    values = basis_values[0, 0]
    potential_cell = potential[0, 0]
    slot_codes = block_lists[0, 0]
    slots = slot_codes.shape[0]
    block_size = values.shape[1] // 9
    weighted = (values.astype(jnp.float32) * potential_cell[:, None]).astype(jnp.bfloat16)
    partial_sums = lax.dot_general(
        weighted, values, (((0,), (0,)), ((), ())), preferred_element_type=jnp.float32
    )
    partial_sums = 0.5 * (partial_sums + partial_sums.T)
    partial_tiles = partial_sums.reshape(3, 3, block_size, 3, 3, block_size)
    extended = extended_2(partial_tiles, (("atoms", 0),), 1, True)
    middle = combine_three(extended[0], extended[2], extended[4], 2)
    extended_line = extended_2(middle, (("grid", 0),), 1, False)
    own_rows = combine_three(extended_line[0], extended_line[2], extended_line[4], 2)
    packed = jnp.stack([own_rows[:, 0:3], own_rows[:, 2:5]])
    arrived = extended_2(packed, (("atoms", 0),), 1, True)
    nearby = jnp.stack([arrived[0], own_rows[:, 1:4], arrived[3]])
    packed_line = jnp.stack([nearby[:, :, :, 0:3], nearby[:, :, :, 2:5]])
    arrived_line = extended_2(packed_line, (("grid", 0),), 1, False)
    gathered = jnp.stack([arrived_line[0], nearby[:, :, :, 1:4], arrived_line[3]], axis=1)
    block_grid = gathered.reshape(9, block_size, 9, block_size)
    selector = (slot_codes[:, None] == jnp.arange(9, dtype=jnp.int32)[None, :]).astype(jnp.float32)
    picked_rows = jnp.einsum("sk,kimj->simj", selector, block_grid, precision=lax.Precision.HIGHEST)
    submatrix = jnp.einsum("simj,tm->sitj", picked_rows, selector, precision=lax.Precision.HIGHEST)
    pieces = [submatrix[k, :, k:].transpose(1, 0, 2).reshape(-1, block_size) for k in range(slots)]
    used = (slot_codes >= 0).astype(jnp.int32)
    source = jnp.where(slot_codes >= 0, jnp.arange(slots, dtype=jnp.int32), -1)
    none = jnp.zeros((1,), jnp.int32)
    meta = jnp.concatenate([jnp.sum(used)[None], none, used, source, none])
    return sign_columns(meta, pieces, lambda k, l: [((k, l - k),)], slots, block_size, 0)[None, None]


def solution(mesh):
    placed = (P("atoms", "grid", None, None), P("atoms", "grid", None), P("atoms", "grid", None))
    dense = mesh.shape["grid"] == 2 and mesh.shape["atoms"] % 2 == 0 and mesh.shape["atoms"] > 4

    def body(basis_values, potential, block_lists):
        if dense and block_lists.shape[2] == REACH * mesh.shape["grid"]:
            return shards_dense_line(basis_values, potential, block_lists)
        return shards(basis_values, potential, block_lists)

    return jax.shard_map(
        body,
        mesh=mesh,
        in_specs=placed,
        out_specs=P("atoms", "grid", None, None),
        check_vma=False,
    )
```

```python
import functools

import jax
import jax.numpy as jnp
from jax import lax
from jax.experimental import pallas as pl
from jax.experimental.pallas import tpu as pltpu
from jax.sharding import PartitionSpec as P

F32 = jnp.float32
BF16 = jnp.bfloat16
REACH = 3
KERNEL_BYTES = 32 * 1024 * 1024
LOADING_BYTES = 46 * 1024 * 1024


def ring(peers, wrap):
    up = [(i, (i + 1) % peers) for i in range(peers if wrap else peers - 1)]
    return up, [(j, i) for i, j in up]


def extended_2(shard, sides, width, wrap):
    for axis, dim in sides:
        peers, length = (lax.axis_size(axis), shard.shape[dim])
        up, down = ring(peers, wrap)
        last = lax.slice_in_dim(shard, length - width, length, axis=dim)
        first = lax.slice_in_dim(shard, 0, width, axis=dim)
        before = lax.ppermute(last, axis, up)
        after = lax.ppermute(first, axis, down)
        shard = jnp.concatenate([before, shard, after], axis=dim)
    return shard


def combine_three(below_part, centre_part, above_part, dim_index):

    def place(portion, before):
        widths = [(0, 0)] * portion.ndim
        widths[dim_index] = (before, 2 - before)
        return jnp.pad(portion, widths)

    return place(below_part, 0) + place(centre_part, 1) + place(above_part, 2)


def give(outs, both_pairs, odd, means, part, block):
    wanted = sorted({pair for lists in both_pairs for pairs in lists for pair in pairs})
    for n, (i, j) in enumerate(wanted):
        means[n] = 0.5 * (part(i, j) + part(j, i).T)
    for out, evens, odds in zip(outs, *both_pairs):
        for n, (even_pair, odd_pair) in enumerate(zip(evens, odds)):
            index = wanted.index(even_pair)
            if even_pair != odd_pair:
                index = jnp.where(odd, wanted.index(odd_pair), index)
            out[n * block : (n + 1) * block, :] = means[index]


def load_kernel(both_pairs, lines, start_ref, values_ref, potential_ref, *refs):
    outs, (held, turned, ends, means, levels, sems, level_sem) = refs[:-7], refs[-7:]
    wide = held.shape[2]
    block = wide // lines
    start = start_ref[0]
    level_copy = pltpu.make_async_copy(potential_ref.at[0], levels, level_sem)
    level_copy.start()
    copies = {}
    for a in (0, 2, 1):
        columns = pl.ds(pl.multiple_of(a * REACH * block + start * block, block), wide)
        copies[a] = pltpu.make_async_copy(
            values_ref.at[0, 0, :, columns], held.at[a], sems.at[a]
        )
        copies[a].start()
    level_copy.wait()

    def prepare(a):
        copies[a].wait()
        turned[a * wide : (a + 1) * wide, :] = (held[a].T.astype(F32) * levels[...]).astype(BF16)

    def multiply(a, b):
        ends[a // 2, b // 2] = jnp.dot(
            turned[a * wide : (a + 1) * wide, :], held[b], preferred_element_type=F32
        )

    prepare(0)
    multiply(0, 0)
    prepare(2)
    multiply(0, 2)
    multiply(2, 0)
    prepare(1)
    multiply(2, 2)

    def part(i, j):
        (a, r), (b, q) = divmod(i, lines), divmod(j, lines)
        return ends[a // 2, b // 2, pl.ds(r * block, block), pl.ds(q * block, block)]

    give(outs, both_pairs, start_ref[1] == 1, means, part, block)


def rest_kernel(both_pairs, lines, start_ref, held, turned, *refs):
    outs, (total, means) = refs[:-2], refs[-2:]
    wide = held.shape[2]
    block = wide // lines
    for a, (low, high) in ((1, (0, 3)), (0, (1, 2)), (2, (1, 2))):
        rows, columns = pl.ds(low * wide, (high - low) * wide), pl.ds(a * wide, wide)
        total[rows, columns] = jnp.dot(turned[rows, :], held[a], preferred_element_type=F32)

    def part(i, j):
        return total[pl.ds(i * block, block), pl.ds(j * block, block)]

    give(outs, both_pairs, start_ref[1] == 1, means, part, block)


def local_products(values, potential, start, both_pairs, lines):
    points, width = values.shape[2:]
    block = width // (REACH * REACH)
    wide = block * lines
    size = wide * REACH
    vmem = pl.BlockSpec(memory_space=pltpu.VMEM)
    smem = pl.BlockSpec(memory_space=pltpu.SMEM)
    hbm = pl.BlockSpec(memory_space=pltpu.HBM)
    first, rest = ([lists[:3] for lists in both_pairs], [lists[3:] for lists in both_pairs])

    def shapes(lists):
        return [jax.ShapeDtypeStruct((len(pairs) * block, block), F32) for pairs in lists[0]]

    def means(lists):
        return pltpu.VMEM((len({p for ls in lists for ps in ls for p in ps}), block, block), F32)

    params = pltpu.CompilerParams(vmem_limit_bytes=LOADING_BYTES)
    *ends, held, turned = pl.pallas_call(
        functools.partial(load_kernel, first, lines),
        out_shape=shapes(first)
        + [
            jax.ShapeDtypeStruct((REACH, points, wide), BF16),
            jax.ShapeDtypeStruct((size, points), BF16),
        ],
        in_specs=[smem, hbm, hbm],
        out_specs=[vmem] * (len(first[0]) + 2),
        scratch_shapes=[
            pltpu.VMEM((2, 2, wide, wide), F32),
            means(first),
            pltpu.VMEM((1, points), F32),
            pltpu.SemaphoreType.DMA((REACH,)),
            pltpu.SemaphoreType.DMA,
        ],
        compiler_params=params,
        cost_estimate=pl.CostEstimate(
            flops=8 * points * wide * wide, bytes_accessed=2 * points * size, transcendentals=0
        ),
        name="ends",
    )(start, values, potential)
    others = pl.pallas_call(
        functools.partial(rest_kernel, rest, lines),
        out_shape=shapes(rest),
        in_specs=[smem, vmem, vmem],
        out_specs=[vmem] * len(rest[0]),
        scratch_shapes=[pltpu.VMEM((size, size), F32), means(rest)],
        compiler_params=params,
        cost_estimate=pl.CostEstimate(
            flops=10 * points * wide * wide, bytes_accessed=0, transcendentals=0
        ),
        name="others",
    )(start, held, turned)
    return [*ends, *others]


def sign_kernel(slots, block, own_tile, place, meta_ref, *refs):
    pieces, (out_ref, xf, cf, yf, xb, sb, yb) = refs[:-7], refs[-7:]
    size, tile = yf.shape
    tiles, per_tile = size // tile, tile // block
    live_count = (meta_ref[0] * block).astype(F32)
    used = [meta_ref[2 + k].astype(F32) for k in range(slots)]
    eye = (
        lax.broadcasted_iota(jnp.int32, (block, block), 0)
        == lax.broadcasted_iota(jnp.int32, (block, block), 1)
    ).astype(F32)
    dot = functools.partial(jnp.dot, preferred_element_type=F32)
    odd = meta_ref[2 + 2 * slots] == 1

    def at(i, width=tile):
        return pl.ds(i * width, width)

    def read(k, l):
        total = None
        for choices in place(k, l):
            parts = [pieces[piece][n * block : (n + 1) * block, :] for piece, n in choices]
            part = parts[0] if len(parts) == 1 else jnp.where(odd, parts[1], parts[0])
            total = part if total is None else total + part
        return total

    def fold(x):
        return jnp.sum(x.reshape(x.shape[0] // 8, 8, x.shape[1]), axis=0)

    def columns_of(left, right):
        for j in range(tiles):
            yield j, dot(left[: (j + 1) * tile, :], right[:, at(j)])

    def keep(to, j, upper):
        upper = upper.astype(BF16)
        to[: (j + 1) * tile, at(j)] = upper
        for i in range(j):
            to[at(j), at(i)] = upper[i * tile : (i + 1) * tile].T

    trace = jnp.sum(sum(fold(read(k, k) * eye) * used[k] for k in range(slots)))
    mean_level = trace / live_count
    square_sum = jnp.zeros((8, block), F32)
    for k in range(slots):
        for l in range(k, slots):
            part = read(k, l)
            if k == l:
                part = part - mean_level * eye
            part = part * -(used[k] * used[l])
            square_sum = square_sum + fold(part * part) * (1.0 if k == l else 2.0)
            rows, columns = at(k, block), at(l, block)
            xf[rows, columns] = part
            short = part.astype(BF16)
            xb[rows, columns] = short
            if k < l:
                xb[columns, rows] = short.T
                if k // per_tile == l // per_tile:
                    xf[columns, rows] = part.T
    norm = lax.rsqrt(jnp.full((1, 1), jnp.sum(square_sum) + 1e-06, F32)) * jnp.sqrt(
        jnp.full((1, 1), live_count, F32)
    )
    for j, square in columns_of(xb, xb):
        keep(sb, j, square * (norm * norm))
    fourth_sum = jnp.zeros((8, tile), F32)
    for j, fourth in columns_of(sb, sb):
        fourth = fourth * fourth
        fourth_sum = fourth_sum + fold(fourth[j * tile :])
        if j:
            fourth_sum = fourth_sum + 2.0 * fold(fourth[: j * tile])
    for j, cube in columns_of(xb, sb):
        cf[: (j + 1) * tile, at(j)] = cube
    rho = jnp.sqrt(jnp.sqrt(jnp.sqrt(jnp.full((1, 1), jnp.sum(fourth_sum) + 1e-06, F32))))
    inverse = 1.0 / rho
    first = norm * inverse
    for j in range(tiles):
        rows, columns = pl.ds(0, (j + 1) * tile), at(j)
        upper = (1.5 * first) * xf[rows, columns] - (0.5 * first * inverse * inverse) * cf[
            rows, columns
        ]
        xf[rows, columns] = upper
        keep(xb, j, upper)
    for j, square in columns_of(xb, xb):
        keep(sb, j, square)
    for j, cube in columns_of(xb, sb):
        upper = 1.5 * xf[: (j + 1) * tile, at(j)] - 0.5 * cube
        keep(yb, j, upper)
        if j == own_tile:
            yf[: (j + 1) * tile, :] = upper
        elif j > own_tile:
            yf[at(j), :] = upper[own_tile * tile : (own_tile + 1) * tile].T

    columns = yf[:, pl.ds(pl.multiple_of(meta_ref[1] * block, block), block)]

    def thin(v):
        high = v.astype(BF16)
        low = (v - high.astype(F32)).astype(BF16)
        halves = []
        for n, pair in enumerate(((high, low), (low, high))):
            rows = pl.ds(n * size // 2, size // 2)
            both = dot(yb[rows, :], jnp.concatenate(pair, axis=1))
            halves.append(both[:, :block] + both[:, block:])
        return jnp.concatenate(halves, axis=0)

    xf[:, :block] = 1.5 * columns - 0.5 * thin(thin(columns))
    for s in range(slots):
        source = meta_ref[2 + slots + s]
        rows = xf[pl.ds(pl.multiple_of(jnp.maximum(source, 0) * block, block), block), :block]
        rows = jnp.where(source >= 0, rows, 0.0)
        out_ref[s * block : (s + 1) * block, :] = 0.5 * (rows + eye if s == 0 else rows)


def sign_columns(meta, pieces, place, slots, block, own_tile):
    size = slots * block
    tile = block * (2 if slots % 2 == 0 else 1)
    vmem = pl.BlockSpec(memory_space=pltpu.VMEM)
    return pl.pallas_call(
        functools.partial(sign_kernel, slots, block, own_tile, place),
        out_shape=jax.ShapeDtypeStruct((size, block), F32),
        in_specs=[pl.BlockSpec(memory_space=pltpu.SMEM)] + [vmem] * len(pieces),
        out_specs=vmem,
        scratch_shapes=[
            pltpu.VMEM((size, size), F32),
            pltpu.VMEM((size, size), F32),
            pltpu.VMEM((size, tile), F32),
            pltpu.VMEM((size, size), BF16),
            pltpu.VMEM((size, size), BF16),
            pltpu.VMEM((size, size), BF16),
        ],
        compiler_params=pltpu.CompilerParams(vmem_limit_bytes=KERNEL_BYTES),
        cost_estimate=pl.CostEstimate(
            flops=8 * size**3, bytes_accessed=4 * size * size, transcendentals=0
        ),
        name="sign",
    )(meta, *pieces)


def shards_dense_line(basis_values, potential, block_lists):
    codes = block_lists[0, 0]
    lines = lax.axis_size("grid")
    position = lax.axis_index("grid").astype(jnp.int32)
    parity = (lax.axis_index("atoms") % 2).astype(jnp.int32)
    block = basis_values.shape[3] // (REACH * REACH)
    slots = REACH * lines
    regions = lax.axis_size("atoms")
    far = [(i, (i + 1 if i % 2 else i - 1) % regions) for i in range(regions)]
    near = [(i, i - 1 if i % 2 else i + 1) for i in range(regions)]
    line_shifts = [[(i, (i + s) % lines) for i in range(lines)] for s in range(1, lines)]
    start = jnp.stack([1 - position, parity])

    def sent(part, axis, pairs):
        return lax.ppermute(part, axis, pairs)

    def line_parts(part):
        return [sent(part, "grid", shift) for shift in line_shifts]

    half = lines // 2
    triangle = [(r, q) for r in range(lines) for q in range(r, lines)]
    strip = [(r, q) for r in range(half) for q in range(lines)]

    def within(a):
        return [(a * lines + r, a * lines + q) for r, q in triangle]

    def across(a, late):
        first = half if late else 0
        return [(a * lines + first + r, (a + 1) * lines + q) for r, q in strip]

    def pairs_of(odd):
        return (
            within(2 * odd),
            within(2 - 2 * odd),
            [(r, 2 * lines + q) for r in range(lines) for q in range(lines)],
            across(odd, not odd),
            across(1 - odd, odd),
            within(1),
            across(odd, odd) + across(1 - odd, not odd),
        )

    own_to_far, own_to_near, outer, side_to_far, side_to_near, own, side = local_products(
        basis_values, potential, start, (pairs_of(0), pairs_of(1)), lines
    )
    outer_parts = [outer] + line_parts(outer)
    own = own + sent(own_to_far, "atoms", far) + sent(own_to_near, "atoms", near)
    side_far, side_near = sent(side_to_far, "atoms", far), sent(side_to_near, "atoms", near)
    side = side + jnp.concatenate([side_far, side_near])
    own = sum(line_parts(own), own)
    side = sum(line_parts(side), side)
    own_far = sent(own, "atoms", far)
    own_near = sent(own, "atoms", near)
    cut = len(strip) * block
    side_far = sent(side[:cut], "atoms", far)
    side_near = sent(side[cut:], "atoms", near)
    pieces = [own, own_far, own_near, side, side_far, side_near] + outer_parts

    def place(k, l):
        (a, r), (b, q) = divmod(k, lines), divmod(l, lines)
        if a == b:
            n = triangle.index((r, q))
            return [(((1, n), (2, n)), ((0, n),), ((2, n), (1, n)))[a]]
        if b - a == 2:
            return [((piece, r * lines + q),) for piece in range(6, len(pieces))]
        n = strip.index((r % half, q))
        kept, given = ((3, n), (3, len(strip) + n)), ((4, n), (5, n))
        choices = kept if (r < half) == (a == 0) else given
        return [choices if a == 0 else choices[::-1]]

    live = jnp.sum((codes >= 0).astype(jnp.int32))
    source = (codes // REACH) * lines + codes % REACH - 1 + position
    source = jnp.where(codes >= 0, source, -1).astype(jnp.int32)
    blocks = jnp.arange(slots, dtype=jnp.int32)
    used = jnp.sum((source[None, :] == blocks[:, None]).astype(jnp.int32), axis=1)
    meta = jnp.concatenate([live[None], position[None], used, source, parity[None]])
    return sign_columns(meta, pieces, place, slots, block, 1)[None, None]


def shards(basis_values, potential, block_lists):
    values = basis_values[0, 0]
    potential_cell = potential[0, 0]
    slot_codes = block_lists[0, 0]
    slots = slot_codes.shape[0]
    block_size = values.shape[1] // 9
    weighted = (values.astype(jnp.float32) * potential_cell[:, None]).astype(jnp.bfloat16)
    partial_sums = lax.dot_general(
        weighted, values, (((0,), (0,)), ((), ())), preferred_element_type=jnp.float32
    )
    partial_sums = 0.5 * (partial_sums + partial_sums.T)
    partial_tiles = partial_sums.reshape(3, 3, block_size, 3, 3, block_size)
    extended = extended_2(partial_tiles, (("atoms", 0),), 1, True)
    middle = combine_three(extended[0], extended[2], extended[4], 2)
    extended_line = extended_2(middle, (("grid", 0),), 1, False)
    own_rows = combine_three(extended_line[0], extended_line[2], extended_line[4], 2)
    packed = jnp.stack([own_rows[:, 0:3], own_rows[:, 2:5]])
    arrived = extended_2(packed, (("atoms", 0),), 1, True)
    nearby = jnp.stack([arrived[0], own_rows[:, 1:4], arrived[3]])
    packed_line = jnp.stack([nearby[:, :, :, 0:3], nearby[:, :, :, 2:5]])
    arrived_line = extended_2(packed_line, (("grid", 0),), 1, False)
    gathered = jnp.stack([arrived_line[0], nearby[:, :, :, 1:4], arrived_line[3]], axis=1)
    block_grid = gathered.reshape(9, block_size, 9, block_size)
    selector = (slot_codes[:, None] == jnp.arange(9, dtype=jnp.int32)[None, :]).astype(jnp.float32)
    picked_rows = jnp.einsum("sk,kimj->simj", selector, block_grid, precision=lax.Precision.HIGHEST)
    submatrix = jnp.einsum("simj,tm->sitj", picked_rows, selector, precision=lax.Precision.HIGHEST)
    pieces = [submatrix[k, :, k:].transpose(1, 0, 2).reshape(-1, block_size) for k in range(slots)]
    used = (slot_codes >= 0).astype(jnp.int32)
    source = jnp.where(slot_codes >= 0, jnp.arange(slots, dtype=jnp.int32), -1)
    none = jnp.zeros((1,), jnp.int32)
    meta = jnp.concatenate([jnp.sum(used)[None], none, used, source, none])
    return sign_columns(meta, pieces, lambda k, l: [((k, l - k),)], slots, block_size, 0)[None, None]


def solution(mesh):
    placed = (P("atoms", "grid", None, None), P("atoms", "grid", None), P("atoms", "grid", None))
    dense = mesh.shape["grid"] == 2 and mesh.shape["atoms"] % 2 == 0 and mesh.shape["atoms"] > 4

    def body(basis_values, potential, block_lists):
        if dense and block_lists.shape[2] == REACH * mesh.shape["grid"]:
            return shards_dense_line(basis_values, potential, block_lists)
        return shards(basis_values, potential, block_lists)

    return jax.shard_map(
        body,
        mesh=mesh,
        in_specs=placed,
        out_specs=P("atoms", "grid", None, None),
        check_vma=False,
    )
```

```python
import functools

import jax
import jax.numpy as jnp
from jax import lax
from jax.experimental import pallas as pl
from jax.experimental.pallas import tpu as pltpu
from jax.sharding import PartitionSpec as P

F32 = jnp.float32
BF16 = jnp.bfloat16
REACH = 3
KERNEL_BYTES = 32 * 1024 * 1024
LOADING_BYTES = 46 * 1024 * 1024


def ring(peers, wrap):
    up = [(i, (i + 1) % peers) for i in range(peers if wrap else peers - 1)]
    return up, [(j, i) for i, j in up]


def extended_2(shard, sides, width, wrap):
    for axis, dim in sides:
        peers, length = (lax.axis_size(axis), shard.shape[dim])
        up, down = ring(peers, wrap)
        last = lax.slice_in_dim(shard, length - width, length, axis=dim)
        first = lax.slice_in_dim(shard, 0, width, axis=dim)
        before = lax.ppermute(last, axis, up)
        after = lax.ppermute(first, axis, down)
        shard = jnp.concatenate([before, shard, after], axis=dim)
    return shard


def combine_three(below_part, centre_part, above_part, dim_index):

    def place(portion, before):
        widths = [(0, 0)] * portion.ndim
        widths[dim_index] = (before, 2 - before)
        return jnp.pad(portion, widths)

    return place(below_part, 0) + place(centre_part, 1) + place(above_part, 2)


def give(outs, both_pairs, odd, means, part, block):
    wanted = sorted({pair for lists in both_pairs for pairs in lists for pair in pairs})
    for n, (i, j) in enumerate(wanted):
        means[n] = 0.5 * (part(i, j) + part(j, i).T)
    for out, evens, odds in zip(outs, *both_pairs):
        for n, (even_pair, odd_pair) in enumerate(zip(evens, odds)):
            index = wanted.index(even_pair)
            if even_pair != odd_pair:
                index = jnp.where(odd, wanted.index(odd_pair), index)
            out[n * block : (n + 1) * block, :] = means[index]


def load_kernel(both_pairs, lines, start_ref, values_ref, potential_ref, *refs):
    outs, (held, turned, ends, means, levels, sems, level_sem) = refs[:-7], refs[-7:]
    wide = held.shape[2]
    block = wide // lines
    start = start_ref[0]
    level_copy = pltpu.make_async_copy(potential_ref.at[0], levels, level_sem)
    level_copy.start()
    copies = {}
    for a in (0, 2):
        columns = pl.ds(pl.multiple_of(a * REACH * block + start * block, block), wide)
        copies[a] = pltpu.make_async_copy(
            values_ref.at[0, 0, :, columns], held.at[a // 2], sems.at[a // 2]
        )
        copies[a].start()
    level_copy.wait()

    def prepare(a):
        copies[2 * a].wait()
        turned[a * wide : (a + 1) * wide, :] = (held[a].T.astype(F32) * levels[...]).astype(BF16)

    def multiply(a, b):
        ends[a, b] = jnp.dot(
            turned[a * wide : (a + 1) * wide, :], held[b], preferred_element_type=F32
        )

    prepare(0)
    multiply(0, 0)
    prepare(1)
    multiply(0, 1)
    multiply(1, 0)
    multiply(1, 1)

    def part(i, j):
        (a, r), (b, q) = divmod(i, lines), divmod(j, lines)
        return ends[a // 2, b // 2, pl.ds(r * block, block), pl.ds(q * block, block)]

    give(outs, both_pairs, start_ref[1] == 1, means, part, block)


def rest_kernel(both_pairs, lines, start_ref, values_ref, potential_ref, held, turned, *refs):
    outs, (total, means, middle, centre, levels, sems) = refs[:-6], refs[-6:]
    wide = held.shape[2]
    block = wide // lines
    columns = pl.ds(pl.multiple_of(REACH * block + start_ref[0] * block, block), wide)
    copy = pltpu.make_async_copy(values_ref.at[0, 0, :, columns], middle, sems.at[0])
    copy.start()
    level_copy = pltpu.make_async_copy(potential_ref.at[0], levels, sems.at[1])
    level_copy.start()
    level_copy.wait()
    copy.wait()
    centre[...] = (middle[...].T.astype(F32) * levels[...]).astype(BF16)
    inner = pl.ds(wide, wide)
    for a in range(2):
        outer = pl.ds(2 * a * wide, wide)
        total[outer, inner] = jnp.dot(
            turned[a * wide : (a + 1) * wide, :], middle[...], preferred_element_type=F32
        )
        total[inner, outer] = jnp.dot(centre[...], held[a], preferred_element_type=F32)
    total[inner, inner] = jnp.dot(centre[...], middle[...], preferred_element_type=F32)

    def part(i, j):
        return total[pl.ds(i * block, block), pl.ds(j * block, block)]

    give(outs, both_pairs, start_ref[1] == 1, means, part, block)


def local_products(values, potential, start, both_pairs, lines):
    points, width = values.shape[2:]
    block = width // (REACH * REACH)
    wide = block * lines
    size = wide * REACH
    vmem = pl.BlockSpec(memory_space=pltpu.VMEM)
    smem = pl.BlockSpec(memory_space=pltpu.SMEM)
    hbm = pl.BlockSpec(memory_space=pltpu.HBM)
    first, rest = ([lists[:3] for lists in both_pairs], [lists[3:] for lists in both_pairs])

    def shapes(lists):
        return [jax.ShapeDtypeStruct((len(pairs) * block, block), F32) for pairs in lists[0]]

    def means(lists):
        return pltpu.VMEM((len({p for ls in lists for ps in ls for p in ps}), block, block), F32)

    params = pltpu.CompilerParams(vmem_limit_bytes=LOADING_BYTES)
    *ends, held, turned = pl.pallas_call(
        functools.partial(load_kernel, first, lines),
        out_shape=shapes(first)
        + [
            jax.ShapeDtypeStruct((2, points, wide), BF16),
            jax.ShapeDtypeStruct((2 * wide, points), BF16),
        ],
        in_specs=[smem, hbm, hbm],
        out_specs=[vmem] * (len(first[0]) + 2),
        scratch_shapes=[
            pltpu.VMEM((2, 2, wide, wide), F32),
            means(first),
            pltpu.VMEM((1, points), F32),
            pltpu.SemaphoreType.DMA((2,)),
            pltpu.SemaphoreType.DMA,
        ],
        compiler_params=params,
        cost_estimate=pl.CostEstimate(
            flops=8 * points * wide * wide, bytes_accessed=2 * points * size, transcendentals=0
        ),
        name="ends",
    )(start, values, potential)
    others = pl.pallas_call(
        functools.partial(rest_kernel, rest, lines),
        out_shape=shapes(rest),
        in_specs=[smem, hbm, hbm, vmem, vmem],
        out_specs=[vmem] * len(rest[0]),
        scratch_shapes=[
            pltpu.VMEM((size, size), F32),
            means(rest),
            pltpu.VMEM((points, wide), BF16),
            pltpu.VMEM((wide, points), BF16),
            pltpu.VMEM((1, points), F32),
            pltpu.SemaphoreType.DMA((2,)),
        ],
        compiler_params=params,
        cost_estimate=pl.CostEstimate(
            flops=10 * points * wide * wide, bytes_accessed=0, transcendentals=0
        ),
        name="others",
    )(start, values, potential, held, turned)
    return [*ends, *others]


def sign_kernel(slots, block, own_tile, place, meta_ref, *refs):
    pieces, (out_ref, xf, cf, yf, xb, sb, yb) = refs[:-7], refs[-7:]
    size, tile = yf.shape
    tiles, per_tile = size // tile, tile // block
    live_count = (meta_ref[0] * block).astype(F32)
    used = [meta_ref[2 + k].astype(F32) for k in range(slots)]
    eye = (
        lax.broadcasted_iota(jnp.int32, (block, block), 0)
        == lax.broadcasted_iota(jnp.int32, (block, block), 1)
    ).astype(F32)
    dot = functools.partial(jnp.dot, preferred_element_type=F32)
    odd = meta_ref[2 + 2 * slots] == 1

    def at(i, width=tile):
        return pl.ds(i * width, width)

    def read(k, l):
        total = None
        for choices in place(k, l):
            parts = [pieces[piece][n * block : (n + 1) * block, :] for piece, n in choices]
            part = parts[0] if len(parts) == 1 else jnp.where(odd, parts[1], parts[0])
            total = part if total is None else total + part
        return total

    def fold(x):
        return jnp.sum(x.reshape(x.shape[0] // 8, 8, x.shape[1]), axis=0)

    def columns_of(left, right):
        for j in range(tiles):
            yield j, dot(left[: (j + 1) * tile, :], right[:, at(j)])

    def keep(to, j, upper):
        upper = upper.astype(BF16)
        to[: (j + 1) * tile, at(j)] = upper
        for i in range(j):
            to[at(j), at(i)] = upper[i * tile : (i + 1) * tile].T

    trace = jnp.sum(sum(fold(read(k, k) * eye) * used[k] for k in range(slots)))
    mean_level = trace / live_count
    square_sum = jnp.zeros((8, block), F32)
    for k in range(slots):
        for l in range(k, slots):
            part = read(k, l)
            if k == l:
                part = part - mean_level * eye
            part = part * -(used[k] * used[l])
            square_sum = square_sum + fold(part * part) * (1.0 if k == l else 2.0)
            rows, columns = at(k, block), at(l, block)
            xf[rows, columns] = part
            short = part.astype(BF16)
            xb[rows, columns] = short
            if k < l:
                xb[columns, rows] = short.T
                if k // per_tile == l // per_tile:
                    xf[columns, rows] = part.T
    norm = lax.rsqrt(jnp.full((1, 1), jnp.sum(square_sum) + 1e-06, F32)) * jnp.sqrt(
        jnp.full((1, 1), live_count, F32)
    )
    for j, square in columns_of(xb, xb):
        keep(sb, j, square * (norm * norm))
    fourth_sum = jnp.zeros((8, tile), F32)
    for j, fourth in columns_of(sb, sb):
        fourth = fourth * fourth
        fourth_sum = fourth_sum + fold(fourth[j * tile :])
        if j:
            fourth_sum = fourth_sum + 2.0 * fold(fourth[: j * tile])
    for j, cube in columns_of(xb, sb):
        cf[: (j + 1) * tile, at(j)] = cube
    rho = jnp.sqrt(jnp.sqrt(jnp.sqrt(jnp.full((1, 1), jnp.sum(fourth_sum) + 1e-06, F32))))
    inverse = 1.0 / rho
    first = norm * inverse
    for j in range(tiles):
        rows, columns = pl.ds(0, (j + 1) * tile), at(j)
        upper = (1.5 * first) * xf[rows, columns] - (0.5 * first * inverse * inverse) * cf[
            rows, columns
        ]
        xf[rows, columns] = upper
        keep(xb, j, upper)
    for j, square in columns_of(xb, xb):
        keep(sb, j, square)
    for j, cube in columns_of(xb, sb):
        upper = 1.5 * xf[: (j + 1) * tile, at(j)] - 0.5 * cube
        keep(yb, j, upper)
        if j == own_tile:
            yf[: (j + 1) * tile, :] = upper
        elif j > own_tile:
            yf[at(j), :] = upper[own_tile * tile : (own_tile + 1) * tile].T

    columns = yf[:, pl.ds(pl.multiple_of(meta_ref[1] * block, block), block)]

    def thin(v):
        high = v.astype(BF16)
        low = (v - high.astype(F32)).astype(BF16)
        halves = []
        for n, pair in enumerate(((high, low), (low, high))):
            rows = pl.ds(n * size // 2, size // 2)
            both = dot(yb[rows, :], jnp.concatenate(pair, axis=1))
            halves.append(both[:, :block] + both[:, block:])
        return jnp.concatenate(halves, axis=0)

    xf[:, :block] = 1.5 * columns - 0.5 * thin(thin(columns))
    for s in range(slots):
        source = meta_ref[2 + slots + s]
        rows = xf[pl.ds(pl.multiple_of(jnp.maximum(source, 0) * block, block), block), :block]
        rows = jnp.where(source >= 0, rows, 0.0)
        out_ref[s * block : (s + 1) * block, :] = 0.5 * (rows + eye if s == 0 else rows)


def sign_columns(meta, pieces, place, slots, block, own_tile):
    size = slots * block
    tile = block * (2 if slots % 2 == 0 else 1)
    vmem = pl.BlockSpec(memory_space=pltpu.VMEM)
    return pl.pallas_call(
        functools.partial(sign_kernel, slots, block, own_tile, place),
        out_shape=jax.ShapeDtypeStruct((size, block), F32),
        in_specs=[pl.BlockSpec(memory_space=pltpu.SMEM)] + [vmem] * len(pieces),
        out_specs=vmem,
        scratch_shapes=[
            pltpu.VMEM((size, size), F32),
            pltpu.VMEM((size, size), F32),
            pltpu.VMEM((size, tile), F32),
            pltpu.VMEM((size, size), BF16),
            pltpu.VMEM((size, size), BF16),
            pltpu.VMEM((size, size), BF16),
        ],
        compiler_params=pltpu.CompilerParams(vmem_limit_bytes=KERNEL_BYTES),
        cost_estimate=pl.CostEstimate(
            flops=8 * size**3, bytes_accessed=4 * size * size, transcendentals=0
        ),
        name="sign",
    )(meta, *pieces)


def shards_dense_line(basis_values, potential, block_lists):
    codes = block_lists[0, 0]
    lines = lax.axis_size("grid")
    position = lax.axis_index("grid").astype(jnp.int32)
    parity = (lax.axis_index("atoms") % 2).astype(jnp.int32)
    block = basis_values.shape[3] // (REACH * REACH)
    slots = REACH * lines
    regions = lax.axis_size("atoms")
    far = [(i, (i + 1 if i % 2 else i - 1) % regions) for i in range(regions)]
    near = [(i, i - 1 if i % 2 else i + 1) for i in range(regions)]
    line_shifts = [[(i, (i + s) % lines) for i in range(lines)] for s in range(1, lines)]
    start = jnp.stack([1 - position, parity])

    def sent(part, axis, pairs):
        return lax.ppermute(part, axis, pairs)

    def line_parts(part):
        return [sent(part, "grid", shift) for shift in line_shifts]

    half = lines // 2
    triangle = [(r, q) for r in range(lines) for q in range(r, lines)]
    strip = [(r, q) for r in range(half) for q in range(lines)]

    def within(a):
        return [(a * lines + r, a * lines + q) for r, q in triangle]

    def across(a, late):
        first = half if late else 0
        return [(a * lines + first + r, (a + 1) * lines + q) for r, q in strip]

    def pairs_of(odd):
        return (
            within(2 * odd),
            within(2 - 2 * odd),
            [(r, 2 * lines + q) for r in range(lines) for q in range(lines)],
            across(odd, not odd),
            across(1 - odd, odd),
            within(1),
            across(odd, odd) + across(1 - odd, not odd),
        )

    own_to_far, own_to_near, outer, side_to_far, side_to_near, own, side = local_products(
        basis_values, potential, start, (pairs_of(0), pairs_of(1)), lines
    )
    outer_parts = [outer] + line_parts(outer)
    own = own + sent(own_to_far, "atoms", far) + sent(own_to_near, "atoms", near)
    side_far, side_near = sent(side_to_far, "atoms", far), sent(side_to_near, "atoms", near)
    side = side + jnp.concatenate([side_far, side_near])
    own = sum(line_parts(own), own)
    side = sum(line_parts(side), side)
    own_far = sent(own, "atoms", far)
    own_near = sent(own, "atoms", near)
    cut = len(strip) * block
    side_far = sent(side[:cut], "atoms", far)
    side_near = sent(side[cut:], "atoms", near)
    pieces = [own, own_far, own_near, side, side_far, side_near] + outer_parts

    def place(k, l):
        (a, r), (b, q) = divmod(k, lines), divmod(l, lines)
        if a == b:
            n = triangle.index((r, q))
            return [(((1, n), (2, n)), ((0, n),), ((2, n), (1, n)))[a]]
        if b - a == 2:
            return [((piece, r * lines + q),) for piece in range(6, len(pieces))]
        n = strip.index((r % half, q))
        kept, given = ((3, n), (3, len(strip) + n)), ((4, n), (5, n))
        choices = kept if (r < half) == (a == 0) else given
        return [choices if a == 0 else choices[::-1]]

    live = jnp.sum((codes >= 0).astype(jnp.int32))
    source = (codes // REACH) * lines + codes % REACH - 1 + position
    source = jnp.where(codes >= 0, source, -1).astype(jnp.int32)
    blocks = jnp.arange(slots, dtype=jnp.int32)
    used = jnp.sum((source[None, :] == blocks[:, None]).astype(jnp.int32), axis=1)
    meta = jnp.concatenate([live[None], position[None], used, source, parity[None]])
    return sign_columns(meta, pieces, place, slots, block, 1)[None, None]


def shards(basis_values, potential, block_lists):
    values = basis_values[0, 0]
    potential_cell = potential[0, 0]
    slot_codes = block_lists[0, 0]
    slots = slot_codes.shape[0]
    block_size = values.shape[1] // 9
    weighted = (values.astype(jnp.float32) * potential_cell[:, None]).astype(jnp.bfloat16)
    partial_sums = lax.dot_general(
        weighted, values, (((0,), (0,)), ((), ())), preferred_element_type=jnp.float32
    )
    partial_sums = 0.5 * (partial_sums + partial_sums.T)
    partial_tiles = partial_sums.reshape(3, 3, block_size, 3, 3, block_size)
    extended = extended_2(partial_tiles, (("atoms", 0),), 1, True)
    middle = combine_three(extended[0], extended[2], extended[4], 2)
    extended_line = extended_2(middle, (("grid", 0),), 1, False)
    own_rows = combine_three(extended_line[0], extended_line[2], extended_line[4], 2)
    packed = jnp.stack([own_rows[:, 0:3], own_rows[:, 2:5]])
    arrived = extended_2(packed, (("atoms", 0),), 1, True)
    nearby = jnp.stack([arrived[0], own_rows[:, 1:4], arrived[3]])
    packed_line = jnp.stack([nearby[:, :, :, 0:3], nearby[:, :, :, 2:5]])
    arrived_line = extended_2(packed_line, (("grid", 0),), 1, False)
    gathered = jnp.stack([arrived_line[0], nearby[:, :, :, 1:4], arrived_line[3]], axis=1)
    block_grid = gathered.reshape(9, block_size, 9, block_size)
    selector = (slot_codes[:, None] == jnp.arange(9, dtype=jnp.int32)[None, :]).astype(jnp.float32)
    picked_rows = jnp.einsum("sk,kimj->simj", selector, block_grid, precision=lax.Precision.HIGHEST)
    submatrix = jnp.einsum("simj,tm->sitj", picked_rows, selector, precision=lax.Precision.HIGHEST)
    pieces = [submatrix[k, :, k:].transpose(1, 0, 2).reshape(-1, block_size) for k in range(slots)]
    used = (slot_codes >= 0).astype(jnp.int32)
    source = jnp.where(slot_codes >= 0, jnp.arange(slots, dtype=jnp.int32), -1)
    none = jnp.zeros((1,), jnp.int32)
    meta = jnp.concatenate([jnp.sum(used)[None], none, used, source, none])
    return sign_columns(meta, pieces, lambda k, l: [((k, l - k),)], slots, block_size, 0)[None, None]


def solution(mesh):
    placed = (P("atoms", "grid", None, None), P("atoms", "grid", None), P("atoms", "grid", None))
    dense = mesh.shape["grid"] == 2 and mesh.shape["atoms"] % 2 == 0 and mesh.shape["atoms"] > 4

    def body(basis_values, potential, block_lists):
        if dense and block_lists.shape[2] == REACH * mesh.shape["grid"]:
            return shards_dense_line(basis_values, potential, block_lists)
        return shards(basis_values, potential, block_lists)

    return jax.shard_map(
        body,
        mesh=mesh,
        in_specs=placed,
        out_specs=P("atoms", "grid", None, None),
        check_vma=False,
    )
```
